32 devices in a mesh: rad: 8 (over z, y), mode: 4 (over x, core).
Axes of the slice: x: 2, y: 2, z: 4, core: 2. Of those that a mesh axis runs over, the one named last changes fastest.
Arguments:
- coefficients: bfloat16 [3, 2, 256, 8, 4, 1152], P(None, None, 'rad', None, 'mode'), may hold values from -6 to 6
- legendre: bfloat16 [8, 4, 1152, 2048], P('rad', 'mode'), may hold values from -0.25 to 0.25
- radial_left_factor: float32 [3, 256, 256], replicated, may hold values from -0.375 to 0.375
- radial_right: float32 [3, 256, 256], replicated, may hold values from -0.375 to 0.375
- eigen_rates: float32 [3, 256], replicated, may hold values from 0.02 to 4
- diffusivity: float32 [3], replicated, may hold values from 0.5 to 4
- slot_order: int32 [8, 4, 2], P('rad', 'mode'), may hold values from 0 to 1023, as said below
- slot_start: int32 [8, 4, 2], P('rad', 'mode'), may hold values from 0 to 1024, as said below
Outputs:
- physical: bfloat16 [3, 2, 8, 4, 256, 2, 2048], P(None, None, None, None, 'rad', None, 'mode')
The draws below stay inside these ranges and needn't reach their ends.
Inputs may be any that keep to these rules, and one draw needn't show every extreme that they name: `slot_order`: the 64 orders are distinct, 0 and 1023 among them; the two rows of every group have block counts 1024 / 128 - floor(m / 128) that add up to exactly 9. `slot_start`: in every group the first row starts at slot 0 and the second at 128 times the first row's block count.
All inputs are finite; a program needn't handle non-finite values.
Results may differ from the reference program's by a relative error of at most 0.0049.
Values may be sent and summed in bfloat16 or wider, within the bound.
A program may use at most 256 MiB of HBM per device.

```python
import math
import jax
import jax.numpy as jnp
from jax import lax

DEGREES = 1024
BLOCK = 128
RADII = 256
LATS = 2048
RAD_COUNT = 8
MODE_COUNT = 4
PACKED = 1152
ROWS = 64
STRIDE = 16


def dealt_table(key):
    offset_key = jax.random.fold_in(key, 11)
    pairing_key = jax.random.fold_in(key, 12)
    flip_key = jax.random.fold_in(key, 13)
    position = jnp.arange(ROWS, dtype=jnp.int32)
    offsets = jax.random.randint(offset_key, (ROWS,), 0, STRIDE, dtype=jnp.int32)
    offsets = jnp.where(position == 0, 0, offsets)
    offsets = jnp.where(position == ROWS - 1, STRIDE - 1, offsets)
    orders_all = STRIDE * position + offsets
    pairing = jax.random.permutation(pairing_key, ROWS // 2).astype(jnp.int32)
    reversed_order = jax.random.randint(flip_key, (ROWS // 2,), 0, 2, dtype=jnp.int32)
    reversed_order = jnp.where(pairing == 0, 0, reversed_order)
    lower_order = orders_all[pairing]
    upper_order = orders_all[ROWS - 1 - pairing]
    leading = jnp.where(reversed_order == 1, upper_order, lower_order)
    trailing = jnp.where(reversed_order == 1, lower_order, upper_order)
    lead_start = jnp.zeros_like(leading)
    trail_start = DEGREES - BLOCK * (leading // BLOCK)
    orders = jnp.stack([leading, trailing], axis=-1).reshape(RAD_COUNT, MODE_COUNT, 2)
    begin_offsets = jnp.stack([lead_start, trail_start], axis=-1).reshape(RAD_COUNT, MODE_COUNT, 2)
    return (orders.astype(jnp.int32), begin_offsets.astype(jnp.int32))


def draw_slot_order(key, part):
    orders, begin_offsets = dealt_table(jax.random.fold_in(key, 5))
    return orders


def draw_slot_start(key, part):
    orders, begin_offsets = dealt_table(jax.random.fold_in(key, 5))
    return begin_offsets


def level_of(stream_key, extent, shards, smallest, high):
    factor_of = 1.0
    for dim, blocks in shards:
        steps = jax.random.uniform(jax.random.fold_in(jax.random.fold_in(stream_key, 6), dim), (blocks,), jnp.float32, smallest / len(shards), high / len(shards))
        factor_of = factor_of * jnp.repeat(jnp.exp(steps), extent[dim] // blocks).reshape((-1,) + (1,) * (len(extent) - 1 - dim))
    return factor_of


def gaussian(stream_key, extent, scale, most, cuts=(), kind=jnp.bfloat16):
    result = scale * jax.random.normal(stream_key, extent, jnp.float32)
    if cuts:
        result = result * level_of(stream_key, extent, cuts, -0.22, 0.18)
    return jnp.clip(result, -most, most).astype(kind)


def setup_inputs(seed: int = 0) -> dict:
    streams_of = jax.random.split(jax.random.key(seed), 9)
    coefficients = gaussian(streams_of[0], (3, 2, RADII, RAD_COUNT, MODE_COUNT, PACKED), 1.0, 6.0, ((2, 8), (4, 4)))
    legendre = gaussian(streams_of[1], (RAD_COUNT, MODE_COUNT, PACKED, LATS), (DEGREES // 2) ** -0.5, 0.25, ((0, 8), (1, 4)))
    radial_left_factor = gaussian(streams_of[2], (3, RADII, RADII), RADII ** -0.5, 0.375, (), jnp.float32)
    radial_right = gaussian(streams_of[3], (3, RADII, RADII), RADII ** -0.5, 0.375, (), jnp.float32)
    eigen_rates = jnp.clip(jnp.exp(jax.random.uniform(streams_of[4], (3, RADII), jnp.float32, math.log(0.02), math.log(4.0))), 0.02, 4.0)
    diffusivity = jnp.clip(jnp.exp(jax.random.uniform(streams_of[5], (3,), jnp.float32, math.log(0.5), math.log(4.0))), 0.5, 4.0)
    slot_order = draw_slot_order(jax.random.fold_in(streams_of[8], 71), 0)
    slot_start = draw_slot_start(jax.random.fold_in(streams_of[8], 71), 0)
    return dict(coefficients=coefficients, legendre=legendre, radial_left_factor=radial_left_factor, radial_right=radial_right, eigen_rates=eigen_rates, diffusivity=diffusivity, slot_order=slot_order, slot_start=slot_start)


def slot_layout(orders, begin_offsets):
    position = jnp.arange(PACKED, dtype=jnp.int32)
    first_degree = (BLOCK * (orders // BLOCK)).astype(jnp.int32)
    row_length = DEGREES - first_degree
    inside = (position[None, :] >= begin_offsets[:, None]) & (position[None, :] < begin_offsets[:, None] + row_length[:, None])
    degree_rows = first_degree[:, None] + position[None, :] - begin_offsets[:, None]
    active_mask = inside & (degree_rows >= orders[:, None])
    degree = jnp.sum(jnp.where(inside, degree_rows, 0), axis=0).astype(jnp.int32)
    return active_mask, degree


def one_group(pieces, radial_left_factor, radial_right, eigen_rates, diffusivity):
    spectral, polynomial_rows, orders, begin_offsets = pieces
    active_mask, degree = slot_layout(orders, begin_offsets)
    degree_level = degree.astype(jnp.float32)
    harmonic = degree_level * (degree_level + 1.0) / (DEGREES * DEGREES)
    shrink = 1.0 + eigen_rates[:, :, None] + diffusivity[:, None, None] * harmonic[None, None, :]
    covered = jnp.any(active_mask, axis=0).astype(jnp.float32)
    factor = covered[None, None, :] / shrink
    field_values = spectral.astype(jnp.float32)
    rotated_view = jnp.einsum("okg,omgx->omkx", radial_left_factor, field_values, precision=lax.Precision.HIGHEST)
    scaled = rotated_view * factor[:, None]
    updated = jnp.einsum("fts,fcsp->fctp", radial_right, scaled, precision=lax.Precision.HIGHEST).astype(jnp.bfloat16)
    per_slot = []
    for slot_index in range(2):
        masked = updated * active_mask[slot_index].astype(jnp.bfloat16)
        summed = jnp.dot(masked.reshape(6 * RADII, PACKED), polynomial_rows, preferred_element_type=jnp.float32)
        per_slot.append(summed.reshape(3, 2, RADII, LATS).astype(jnp.bfloat16))
    return jnp.stack(per_slot, axis=3)


def reference(coefficients, legendre, radial_left_factor, radial_right, eigen_rates, diffusivity, slot_order, slot_start):
    total_group_count = RAD_COUNT * MODE_COUNT
    spectral_groups = jnp.transpose(coefficients, (3, 4, 0, 1, 2, 5)).reshape(total_group_count, 3, 2, RADII, PACKED)
    legendre_groups = legendre.reshape(total_group_count, PACKED, LATS)
    order_groups = slot_order.reshape(total_group_count, 2).astype(jnp.int32)
    start_groups = slot_start.reshape(total_group_count, 2).astype(jnp.int32)
    results = lax.map(lambda pieces: one_group(pieces, radial_left_factor, radial_right, eigen_rates, diffusivity), (spectral_groups, legendre_groups, order_groups, start_groups))
    results = results.reshape(RAD_COUNT, MODE_COUNT, 3, 2, RADII, 2, LATS)
    return jnp.transpose(results, (2, 3, 0, 1, 4, 5, 6))
```

```python
import functools
import jax
import jax.numpy as jnp
from jax import lax
from jax.experimental import pallas as pl
from jax.experimental.pallas import tpu as pltpu
from jax.sharding import PartitionSpec as P

DEGREES = 1024
BLOCK = 128
MESH = pl.DeviceIdType.MESH


def slot_layout(orders, begin_offsets, packed):
    position = jnp.arange(packed, dtype=jnp.int32)
    first_degree = BLOCK * (orders // BLOCK)
    row_length = DEGREES - first_degree
    inside = (position[None, :] >= begin_offsets[:, None]) & (
        position[None, :] < begin_offsets[:, None] + row_length[:, None]
    )
    degree_rows = first_degree[:, None] + position[None, :] - begin_offsets[:, None]
    active_mask = inside & (degree_rows >= orders[:, None])
    degree = jnp.sum(jnp.where(inside, degree_rows, 0), axis=0)
    return (active_mask, degree)


def far_first(count):
    return sorted(range(count), key=lambda k: (-min(k, count - k), k))


def exchange_kernel(rads, modes, u_ref, l_ref, o_ref, held, send_sem, recv_sem, local_sem):
    my_rad = lax.axis_index("rad")
    my_mode = lax.axis_index("mode")
    devices = rads * modes
    parts = u_ref.shape[0]
    rows, lats = held.shape[1], held.shape[3]
    me = my_rad * modes + my_mode

    barrier = pltpu.get_barrier_semaphore()
    for ka in range(rads):
        for kb in range(modes):
            if ka or kb:
                peer = (lax.rem(my_rad + ka, rads), lax.rem(my_mode + kb, modes))
                pl.semaphore_signal(barrier, inc=1, device_id=peer, device_id_type=MESH)
    pl.semaphore_wait(barrier, devices - 1)

    def one_part(c, carry):
        for kb in range(modes):
            b = lax.rem(my_mode + kb, modes)
            columns = pl.ds(pl.multiple_of(b * lats, lats), lats)
            summed = jnp.dot(u_ref[c], l_ref[:, columns], preferred_element_type=jnp.float32)
            blocks = summed.reshape(rads, rows, 2, lats).astype(jnp.bfloat16)
            for a in range(rads):
                held[(c * modes + kb) * rads + a] = blocks[a]
            for ka in far_first(rads):
                a = lax.rem(my_rad + ka, rads)
                source = held.at[(c * modes + kb) * rads + a]
                target = o_ref.at[c * devices + me]
                if ka or kb:
                    pltpu.make_async_remote_copy(
                        src_ref=source,
                        dst_ref=target,
                        send_sem=send_sem,
                        recv_sem=recv_sem,
                        device_id=(a, b),
                        device_id_type=MESH,
                    ).start()
                else:
                    pltpu.make_async_copy(source, target, local_sem).start()
        return carry

    lax.fori_loop(0, parts, one_part, 0)
    remote = pl.ds(0, parts * (devices - 1))
    pltpu.make_async_copy(held.at[remote], held.at[remote], send_sem).wait()
    pltpu.make_async_copy(o_ref.at[remote], o_ref.at[remote], recv_sem).wait()
    own = pl.ds(0, parts)
    pltpu.make_async_copy(held.at[own], o_ref.at[own], local_sem).wait()


def on_device(
    rads,
    modes,
    coefficients,
    legendre,
    radial_left_factor,
    radial_right,
    eigen_rates,
    diffusivity,
    slot_order,
    slot_start,
):
    packed, lats = legendre.shape[2:]
    radii = radial_right.shape[1]
    fields, parts_count = coefficients.shape[:2]
    parts = fields * parts_count
    devices = rads * modes
    active_mask, degree = slot_layout(slot_order.reshape(2), slot_start.reshape(2), packed)
    degree_level = degree.astype(jnp.float32)
    harmonic = degree_level * (degree_level + 1.0) / (DEGREES * DEGREES)
    shrink = 1.0 + eigen_rates[:, :, None] + diffusivity[:, None, None] * harmonic[None, None, :]
    covered = jnp.any(active_mask, axis=0).astype(jnp.float32)
    factor = covered[None, None, :] / shrink
    arrived = lax.all_to_all(coefficients, "rad", split_axis=3, concat_axis=2, tiled=True)
    field_values = arrived.reshape(fields, parts_count, radii, packed)
    turned = jnp.einsum(
        "fkr,fcrp->fckp", radial_left_factor, field_values.astype(jnp.float32), precision=lax.Precision.HIGHEST
    )
    scaled = turned * factor[:, None]
    doubled = jnp.repeat(radial_right, 2, axis=1)
    result = jnp.einsum("ftk,fckp->fctp", doubled, scaled, precision=lax.Precision.HIGHEST)
    row_masks = jnp.tile(active_mask.astype(jnp.bfloat16), (radii, 1))
    updated = (result.astype(jnp.bfloat16) * row_masks).reshape(parts, 2 * radii, packed)
    rows, columns = radii // rads, lats // modes
    landed = pl.pallas_call(
        functools.partial(exchange_kernel, rads, modes),
        out_shape=jax.ShapeDtypeStruct((parts * devices, rows, 2, columns), jnp.bfloat16),
        in_specs=[pl.BlockSpec(memory_space=pltpu.VMEM)] * 2,
        out_specs=pl.BlockSpec(memory_space=pl.ANY),
        scratch_shapes=[
            pltpu.VMEM((parts * devices, rows, 2, columns), jnp.bfloat16),
            pltpu.SemaphoreType.DMA,
            pltpu.SemaphoreType.DMA,
            pltpu.SemaphoreType.DMA,
        ],
        compiler_params=pltpu.CompilerParams(
            collective_id=0, has_side_effects=True, vmem_limit_bytes=60 * 2**20
        ),
    )(updated, legendre.reshape(packed, lats))
    return landed.reshape(fields, parts_count, rads, modes, rows, 2, columns)


def solution(mesh):
    rads, modes = mesh.shape["rad"], mesh.shape["mode"]
    return jax.shard_map(
        functools.partial(on_device, rads, modes),
        mesh=mesh,
        in_specs=(
            P(None, None, "rad", None, "mode", None),
            P("rad", "mode", None, None),
            P(),
            P(),
            P(),
            P(),
            P("rad", "mode", None),
            P("rad", "mode", None),
        ),
        out_specs=P(None, None, None, None, "rad", None, "mode"),
        check_vma=False,
    )
```

```python
import functools
import jax
import jax.numpy as jnp
from jax import lax
from jax.experimental import pallas as pl
from jax.experimental.pallas import tpu as pltpu
from jax.sharding import PartitionSpec as P

DEGREES = 1024
BLOCK = 128
MESH = pl.DeviceIdType.MESH


def far_first(count):
    return sorted(range(count), key=lambda k: (-min(k, count - k), k))


def whole_kernel(
    rads,
    modes,
    parts_count,
    order_ref,
    start_ref,
    diffusivity_ref,
    eigen_ref,
    left_ref,
    right_ref,
    x_ref,
    legendre_ref,
    o_ref,
    arrived,
    polynomial_rows,
    updated,
    held,
    in_send,
    in_recv,
    legendre_sem,
    out_send,
    out_recv,
    out_local,
):
    my_rad = lax.axis_index("rad")
    my_mode = lax.axis_index("mode")
    devices = rads * modes
    parts = arrived.shape[0]
    packed = arrived.shape[3]
    radii = right_ref.shape[1]
    rows, lats = held.shape[1], held.shape[3]
    me = my_rad * modes + my_mode

    fetch = pltpu.make_async_copy(legendre_ref, polynomial_rows, legendre_sem)
    fetch.start()
    barrier = pltpu.get_barrier_semaphore()
    for ka in range(rads):
        for kb in range(modes):
            if ka or kb:
                peer = (lax.rem(my_rad + ka, rads), lax.rem(my_mode + kb, modes))
                pl.semaphore_signal(barrier, inc=1, device_id=peer, device_id_type=MESH)
    pl.semaphore_wait(barrier, devices - 1)

    def send_part(c, carry):
        for ka in far_first(rads):
            a = lax.rem(my_rad + ka, rads)
            source = x_ref.at[a, c]
            target = arrived.at[c, my_rad]
            if ka:
                pltpu.make_async_remote_copy(
                    src_ref=source,
                    dst_ref=target,
                    send_sem=in_send,
                    recv_sem=in_recv.at[c],
                    device_id=(a, my_mode),
                    device_id_type=MESH,
                ).start()
            else:
                pltpu.make_async_copy(source, target, in_recv.at[c]).start()
        return carry

    lax.fori_loop(0, parts, send_part, 0)

    position = lax.broadcasted_iota(jnp.int32, (1, packed), 1)
    live = []
    degree = jnp.zeros((1, packed), jnp.int32)
    for s in range(2):
        order = order_ref[0, 0, s]
        start = start_ref[0, 0, s]
        first_degree = BLOCK * (order // BLOCK)
        inside = (position >= start) & (position < start + DEGREES - first_degree)
        row_degree = first_degree + position - start
        degree = degree + jnp.where(inside, row_degree, 0)
        live.append(jnp.where(inside & (row_degree >= order), 1.0, 0.0).astype(jnp.float32))
    degree_level = degree.astype(jnp.float32)
    harmonic = degree_level * (degree_level + 1.0) / (DEGREES * DEGREES)
    covered = jnp.maximum(live[0], live[1])
    row = lax.broadcasted_iota(jnp.int32, (2 * radii, radii), 0)
    column = lax.broadcasted_iota(jnp.int32, (2 * radii, radii), 1)
    doubling = jnp.where(row // 2 == column, 1.0, 0.0).astype(jnp.bfloat16)
    parity = lax.broadcasted_iota(jnp.int32, (2 * radii, packed), 0) % 2
    fetch.wait()

    def one_part(c, carry):
        field = c // parts_count
        pltpu.make_async_copy(arrived.at[c], arrived.at[c], in_recv.at[c]).wait()
        rates = eigen_ref[pl.ds(field, 1), :]
        rates = jnp.transpose(jnp.broadcast_to(rates, (128, radii)))[:, 0:1]
        shrink = 1.0 + rates + diffusivity_ref[field] * harmonic
        values = arrived[c].reshape(radii, packed).astype(jnp.float32)
        turned = jnp.dot(
            left_ref[field], values, precision=lax.Precision.HIGHEST, preferred_element_type=jnp.float32
        )
        scaled = turned * (covered / shrink)
        result = jnp.dot(
            right_ref[field], scaled, precision=lax.Precision.HIGHEST, preferred_element_type=jnp.float32
        )
        doubled = jnp.dot(doubling, result.astype(jnp.bfloat16), preferred_element_type=jnp.float32)
        updated[...] = (doubled * jnp.where(parity == 0, live[0], live[1])).astype(jnp.bfloat16)
        for kb in range(modes):
            b = lax.rem(my_mode + kb, modes)
            columns = pl.ds(pl.multiple_of(b * lats, lats), lats)
            summed = jnp.dot(
                updated[...], polynomial_rows[:, columns], preferred_element_type=jnp.float32
            )
            blocks = summed.reshape(rads, rows, 2, lats).astype(jnp.bfloat16)
            for a in range(rads):
                held[(c * modes + kb) * rads + a] = blocks[a]
            for ka in far_first(rads):
                a = lax.rem(my_rad + ka, rads)
                source = held.at[(c * modes + kb) * rads + a]
                target = o_ref.at[c * devices + me]
                if ka or kb:
                    pltpu.make_async_remote_copy(
                        src_ref=source,
                        dst_ref=target,
                        send_sem=out_send,
                        recv_sem=out_recv,
                        device_id=(a, b),
                        device_id_type=MESH,
                    ).start()
                else:
                    pltpu.make_async_copy(source, target, out_local).start()
        return carry

    lax.fori_loop(0, parts, one_part, 0)
    others = arrived.at[:, pl.ds(0, rads - 1)]
    pltpu.make_async_copy(others, others, in_send).wait()
    remote = pl.ds(0, parts * (devices - 1))
    pltpu.make_async_copy(held.at[remote], held.at[remote], out_send).wait()
    pltpu.make_async_copy(o_ref.at[remote], o_ref.at[remote], out_recv).wait()
    own = pl.ds(0, parts)
    pltpu.make_async_copy(held.at[own], o_ref.at[own], out_local).wait()


def on_device(
    rads,
    modes,
    coefficients,
    legendre,
    radial_left_factor,
    radial_right,
    eigen_rates,
    diffusivity,
    slot_order,
    slot_start,
):
    packed, lats = legendre.shape[2:]
    radii = radial_right.shape[1]
    fields, parts_count = coefficients.shape[:2]
    parts = fields * parts_count
    devices = rads * modes
    rows, columns = radii // rads, lats // modes
    outgoing = jnp.transpose(
        coefficients.reshape(parts, rows, rads, packed), (2, 0, 1, 3)
    )
    smem = pl.BlockSpec(memory_space=pltpu.SMEM)
    vmem = pl.BlockSpec(memory_space=pltpu.VMEM)
    hbm = pl.BlockSpec(memory_space=pltpu.HBM)
    landed = pl.pallas_call(
        functools.partial(whole_kernel, rads, modes, parts_count),
        out_shape=jax.ShapeDtypeStruct((parts * devices, rows, 2, columns), jnp.bfloat16),
        in_specs=[smem, smem, smem, vmem, vmem, vmem, hbm, hbm],
        out_specs=pl.BlockSpec(memory_space=pl.ANY),
        scratch_shapes=[
            pltpu.VMEM((parts, rads, rows, packed), jnp.bfloat16),
            pltpu.VMEM((packed, lats), jnp.bfloat16),
            pltpu.VMEM((2 * radii, packed), jnp.bfloat16),
            pltpu.VMEM((parts * devices, rows, 2, columns), jnp.bfloat16),
            pltpu.SemaphoreType.DMA,
            pltpu.SemaphoreType.DMA((parts,)),
            pltpu.SemaphoreType.DMA,
            pltpu.SemaphoreType.DMA,
            pltpu.SemaphoreType.DMA,
            pltpu.SemaphoreType.DMA,
        ],
        compiler_params=pltpu.CompilerParams(
            collective_id=0, has_side_effects=True, vmem_limit_bytes=40 * 2**20
        ),
    )(
        slot_order,
        slot_start,
        diffusivity,
        eigen_rates,
        radial_left_factor,
        radial_right,
        outgoing,
        legendre.reshape(packed, lats),
    )
    return landed.reshape(fields, parts_count, rads, modes, rows, 2, columns)


def solution(mesh):
    rads, modes = mesh.shape["rad"], mesh.shape["mode"]
    return jax.shard_map(
        functools.partial(on_device, rads, modes),
        mesh=mesh,
        in_specs=(
            P(None, None, "rad", None, "mode", None),
            P("rad", "mode", None, None),
            P(),
            P(),
            P(),
            P(),
            P("rad", "mode", None),
            P("rad", "mode", None),
        ),
        out_specs=P(None, None, None, None, "rad", None, "mode"),
        check_vma=False,
    )
```

```python
import functools
import jax
import jax.numpy as jnp
from jax import lax
from jax.experimental import pallas as pl
from jax.experimental.pallas import tpu as pltpu
from jax.sharding import PartitionSpec as P

DEGREES = 1024
BLOCK = 128
MESH = pl.DeviceIdType.MESH


def far_first(count):
    return sorted(range(count), key=lambda k: (-min(k, count - k), k))


def whole_kernel(
    rads,
    modes,
    parts_count,
    order_ref,
    start_ref,
    diffusivity_ref,
    eigen_ref,
    left_hbm,
    right_hbm,
    x_ref,
    legendre_ref,
    o_ref,
    left_ref,
    right_ref,
    entering,
    outgoing,
    arrived,
    polynomial_rows,
    updated,
    held,
    enter_sem,
    in_send,
    in_recv,
    factor_sem,
    legendre_sem,
    out_send,
    out_recv,
    out_local,
):
    my_rad = lax.axis_index("rad")
    my_mode = lax.axis_index("mode")
    devices = rads * modes
    parts = arrived.shape[0]
    packed = arrived.shape[3]
    radii = right_ref.shape[1]
    rows, lats = held.shape[1], held.shape[3]
    me = my_rad * modes + my_mode

    def enter(c):
        return pltpu.make_async_copy(x_ref.at[c], entering.at[c], enter_sem.at[c])

    for c in range(parts):
        enter(c).start()
    fetches = (
        pltpu.make_async_copy(left_hbm, left_ref, factor_sem.at[0]),
        pltpu.make_async_copy(right_hbm, right_ref, factor_sem.at[1]),
        pltpu.make_async_copy(legendre_ref, polynomial_rows, legendre_sem),
    )
    for fetch in fetches:
        fetch.start()
    barrier = pltpu.get_barrier_semaphore()
    for ka in range(rads):
        for kb in range(modes):
            if ka or kb:
                peer = (lax.rem(my_rad + ka, rads), lax.rem(my_mode + kb, modes))
                pl.semaphore_signal(barrier, inc=1, device_id=peer, device_id_type=MESH)

    def turn(c):
        enter(c).wait()
        outgoing[c] = jnp.swapaxes(entering[c], 0, 1)

    turn(0)
    pl.semaphore_wait(barrier, devices - 1)

    def send_part(c, carry):
        @pl.when(c > 0)
        def _():
            turn(c)

        for ka in far_first(rads):
            a = lax.rem(my_rad + ka, rads)
            source = outgoing.at[c, a]
            target = arrived.at[c, my_rad]
            if ka:
                pltpu.make_async_remote_copy(
                    src_ref=source,
                    dst_ref=target,
                    send_sem=in_send,
                    recv_sem=in_recv.at[c],
                    device_id=(a, my_mode),
                    device_id_type=MESH,
                ).start()
            else:
                pltpu.make_async_copy(source, target, in_recv.at[c]).start()
        return carry

    lax.fori_loop(0, parts, send_part, 0)

    position = lax.broadcasted_iota(jnp.int32, (1, packed), 1)
    live = []
    degree = jnp.zeros((1, packed), jnp.int32)
    for s in range(2):
        order = order_ref[0, 0, s]
        start = start_ref[0, 0, s]
        first_degree = BLOCK * (order // BLOCK)
        inside = (position >= start) & (position < start + DEGREES - first_degree)
        row_degree = first_degree + position - start
        degree = degree + jnp.where(inside, row_degree, 0)
        live.append(jnp.where(inside & (row_degree >= order), 1.0, 0.0).astype(jnp.float32))
    degree_level = degree.astype(jnp.float32)
    harmonic = degree_level * (degree_level + 1.0) / (DEGREES * DEGREES)
    covered = jnp.maximum(live[0], live[1])
    row = lax.broadcasted_iota(jnp.int32, (2 * radii, radii), 0)
    column = lax.broadcasted_iota(jnp.int32, (2 * radii, radii), 1)
    doubling = jnp.where(row // 2 == column, 1.0, 0.0).astype(jnp.bfloat16)
    parity = lax.broadcasted_iota(jnp.int32, (2 * radii, packed), 0) % 2
    for fetch in fetches:
        fetch.wait()

    def one_part(c, carry):
        field = c // parts_count
        pltpu.make_async_copy(arrived.at[c], arrived.at[c], in_recv.at[c]).wait()
        rates = eigen_ref[pl.ds(field, 1), :]
        rates = jnp.transpose(jnp.broadcast_to(rates, (128, radii)))[:, 0:1]
        shrink = 1.0 + rates + diffusivity_ref[field] * harmonic
        values = arrived[c].reshape(radii, packed).astype(jnp.float32)
        turned = jnp.dot(
            left_ref[field], values, precision=lax.Precision.HIGHEST, preferred_element_type=jnp.float32
        )
        scaled = turned * (covered / shrink)
        result = jnp.dot(
            right_ref[field], scaled, precision=lax.Precision.HIGHEST, preferred_element_type=jnp.float32
        )
        doubled = jnp.dot(doubling, result.astype(jnp.bfloat16), preferred_element_type=jnp.float32)
        updated[...] = (doubled * jnp.where(parity == 0, live[0], live[1])).astype(jnp.bfloat16)
        for kb in range(modes):
            b = lax.rem(my_mode + kb, modes)
            columns = pl.ds(pl.multiple_of(b * lats, lats), lats)
            summed = jnp.dot(
                updated[...], polynomial_rows[:, columns], preferred_element_type=jnp.float32
            )
            blocks = summed.reshape(rads, rows, 2, lats).astype(jnp.bfloat16)
            for a in range(rads):
                held[(c * modes + kb) * rads + a] = blocks[a]
            for ka in far_first(rads):
                a = lax.rem(my_rad + ka, rads)
                source = held.at[(c * modes + kb) * rads + a]
                target = o_ref.at[c * devices + me]
                if ka or kb:
                    pltpu.make_async_remote_copy(
                        src_ref=source,
                        dst_ref=target,
                        send_sem=out_send,
                        recv_sem=out_recv,
                        device_id=(a, b),
                        device_id_type=MESH,
                    ).start()
                else:
                    pltpu.make_async_copy(source, target, out_local).start()
        return carry

    lax.fori_loop(0, parts, one_part, 0)
    others = arrived.at[:, pl.ds(0, rads - 1)]
    pltpu.make_async_copy(others, others, in_send).wait()
    remote = pl.ds(0, parts * (devices - 1))
    pltpu.make_async_copy(held.at[remote], held.at[remote], out_send).wait()
    pltpu.make_async_copy(o_ref.at[remote], o_ref.at[remote], out_recv).wait()
    own = pl.ds(0, parts)
    pltpu.make_async_copy(held.at[own], o_ref.at[own], out_local).wait()


def on_device(
    rads,
    modes,
    coefficients,
    legendre,
    radial_left_factor,
    radial_right,
    eigen_rates,
    diffusivity,
    slot_order,
    slot_start,
):
    packed, lats = legendre.shape[2:]
    radii = radial_right.shape[1]
    fields, parts_count = coefficients.shape[:2]
    parts = fields * parts_count
    devices = rads * modes
    rows, columns = radii // rads, lats // modes
    smem = pl.BlockSpec(memory_space=pltpu.SMEM)
    vmem = pl.BlockSpec(memory_space=pltpu.VMEM)
    hbm = pl.BlockSpec(memory_space=pltpu.HBM)
    landed = pl.pallas_call(
        functools.partial(whole_kernel, rads, modes, parts_count),
        out_shape=pltpu.VMEM((parts * devices, rows, 2, columns), jnp.bfloat16),
        in_specs=[smem, smem, smem, vmem, hbm, hbm, hbm, hbm],
        out_specs=pl.BlockSpec(memory_space=pl.ANY),
        scratch_shapes=[
            pltpu.VMEM(radial_left_factor.shape, jnp.float32),
            pltpu.VMEM(radial_right.shape, jnp.float32),
            pltpu.VMEM((parts, rows, rads, packed), jnp.bfloat16),
            pltpu.VMEM((parts, rads, rows, packed), jnp.bfloat16),
            pltpu.VMEM((parts, rads, rows, packed), jnp.bfloat16),
            pltpu.VMEM((packed, lats), jnp.bfloat16),
            pltpu.VMEM((2 * radii, packed), jnp.bfloat16),
            pltpu.VMEM((parts * devices, rows, 2, columns), jnp.bfloat16),
            pltpu.SemaphoreType.DMA((parts,)),
            pltpu.SemaphoreType.DMA,
            pltpu.SemaphoreType.DMA((parts,)),
            pltpu.SemaphoreType.DMA((2,)),
            pltpu.SemaphoreType.DMA,
            pltpu.SemaphoreType.DMA,
            pltpu.SemaphoreType.DMA,
            pltpu.SemaphoreType.DMA,
        ],
        compiler_params=pltpu.CompilerParams(
            collective_id=0, has_side_effects=True, vmem_limit_bytes=46 * 2**20
        ),
    )(
        slot_order,
        slot_start,
        diffusivity,
        eigen_rates,
        radial_left_factor,
        radial_right,
        coefficients.reshape(parts, rows, rads, packed),
        legendre.reshape(packed, lats),
    )
    return landed.reshape(fields, parts_count, rads, modes, rows, 2, columns)


def solution(mesh):
    rads, modes = mesh.shape["rad"], mesh.shape["mode"]
    return jax.shard_map(
        functools.partial(on_device, rads, modes),
        mesh=mesh,
        in_specs=(
            P(None, None, "rad", None, "mode", None),
            P("rad", "mode", None, None),
            P(),
            P(),
            P(),
            P(),
            P("rad", "mode", None),
            P("rad", "mode", None),
        ),
        out_specs=P(None, None, None, None, "rad", None, "mode"),
        check_vma=False,
    )
```

```python
import functools
import jax
import jax.numpy as jnp
from jax import lax
from jax.experimental import pallas as pl
from jax.experimental.pallas import tpu as pltpu
from jax.sharding import PartitionSpec as P

DEGREES = 1024
BLOCK = 128
MESH = pl.DeviceIdType.MESH


def peer_rad(my_rad, rads, k):
    half = rads // 2
    near = my_rad // half
    side = near if k < half else 1 - near
    return side * half + lax.rem(my_rad % half + k, half)


def whole_kernel(
    rads,
    modes,
    parts_count,
    order_ref,
    start_ref,
    diffusivity_ref,
    eigen_ref,
    left_hbm,
    right_hbm,
    x_ref,
    legendre_ref,
    o_ref,
    left_ref,
    right_ref,
    entering,
    outgoing,
    arrived,
    polynomial_rows,
    updated,
    held,
    enter_sem,
    in_send,
    in_recv,
    factor_sem,
    legendre_sem,
    out_send,
    out_recv,
    out_local,
):
    my_rad = lax.axis_index("rad")
    my_mode = lax.axis_index("mode")
    devices = rads * modes
    parts = arrived.shape[0]
    packed = arrived.shape[3]
    radii = right_ref.shape[1]
    rows, lats = held.shape[1], held.shape[3]
    me = my_rad * modes + my_mode

    def enter(c):
        return pltpu.make_async_copy(x_ref.at[c], entering.at[c], enter_sem.at[c])

    for c in range(parts):
        enter(c).start()
    fetches = (
        pltpu.make_async_copy(left_hbm, left_ref, factor_sem.at[0]),
        pltpu.make_async_copy(right_hbm, right_ref, factor_sem.at[1]),
        pltpu.make_async_copy(legendre_ref, polynomial_rows, legendre_sem),
    )
    for fetch in fetches:
        fetch.start()
    barrier = pltpu.get_barrier_semaphore()
    for ka in range(rads):
        for kb in range(modes):
            if ka or kb:
                peer = (lax.rem(my_rad + ka, rads), lax.rem(my_mode + kb, modes))
                pl.semaphore_signal(barrier, inc=1, device_id=peer, device_id_type=MESH)

    def turn(c):
        enter(c).wait()
        outgoing[c] = jnp.swapaxes(entering[c], 0, 1)

    turn(0)
    pl.semaphore_wait(barrier, devices - 1)

    def send_part(c, carry):
        @pl.when(c > 0)
        def _():
            turn(c)

        for ka in range(rads):
            a = peer_rad(my_rad, rads, ka)
            source = outgoing.at[c, a]
            target = arrived.at[c, my_rad]
            if ka:
                pltpu.make_async_remote_copy(
                    src_ref=source,
                    dst_ref=target,
                    send_sem=in_send,
                    recv_sem=in_recv.at[c],
                    device_id=(a, my_mode),
                    device_id_type=MESH,
                ).start()
            else:
                pltpu.make_async_copy(source, target, in_recv.at[c]).start()
        return carry

    lax.fori_loop(0, parts, send_part, 0)

    position = lax.broadcasted_iota(jnp.int32, (1, packed), 1)
    live = []
    degree = jnp.zeros((1, packed), jnp.int32)
    for s in range(2):
        order = order_ref[0, 0, s]
        start = start_ref[0, 0, s]
        first_degree = BLOCK * (order // BLOCK)
        inside = (position >= start) & (position < start + DEGREES - first_degree)
        row_degree = first_degree + position - start
        degree = degree + jnp.where(inside, row_degree, 0)
        live.append(jnp.where(inside & (row_degree >= order), 1.0, 0.0).astype(jnp.float32))
    degree_level = degree.astype(jnp.float32)
    harmonic = degree_level * (degree_level + 1.0) / (DEGREES * DEGREES)
    covered = jnp.maximum(live[0], live[1])
    row = lax.broadcasted_iota(jnp.int32, (2 * radii, radii), 0)
    column = lax.broadcasted_iota(jnp.int32, (2 * radii, radii), 1)
    doubling = jnp.where(row // 2 == column, 1.0, 0.0).astype(jnp.bfloat16)
    parity = lax.broadcasted_iota(jnp.int32, (2 * radii, packed), 0) % 2
    for fetch in fetches:
        fetch.wait()

    def one_part(c, carry):
        field = c // parts_count
        pltpu.make_async_copy(arrived.at[c], arrived.at[c], in_recv.at[c]).wait()
        rates = eigen_ref[pl.ds(field, 1), :]
        rates = jnp.transpose(jnp.broadcast_to(rates, (128, radii)))[:, 0:1]
        shrink = 1.0 + rates + diffusivity_ref[field] * harmonic
        values = arrived[c].reshape(radii, packed).astype(jnp.float32)
        turned = jnp.dot(
            left_ref[field], values, precision=lax.Precision.HIGHEST, preferred_element_type=jnp.float32
        )
        scaled = turned * (covered / shrink)
        result = jnp.dot(
            right_ref[field], scaled, precision=lax.Precision.HIGHEST, preferred_element_type=jnp.float32
        )
        doubled = jnp.dot(doubling, result.astype(jnp.bfloat16), preferred_element_type=jnp.float32)
        updated[...] = (doubled * jnp.where(parity == 0, live[0], live[1])).astype(jnp.bfloat16)
        for kb in range(modes):
            b = lax.rem(my_mode + kb, modes)
            columns = pl.ds(pl.multiple_of(b * lats, lats), lats)
            summed = jnp.dot(
                updated[...], polynomial_rows[:, columns], preferred_element_type=jnp.float32
            )
            blocks = summed.reshape(rads, rows, 2, lats).astype(jnp.bfloat16)
            for a in range(rads):
                held[(c * modes + kb) * rads + a] = blocks[a]
        for ka in range(rads):
            for kb in range(modes):
                a = peer_rad(my_rad, rads, ka)
                b = lax.rem(my_mode + kb, modes)
                source = held.at[(c * modes + kb) * rads + a]
                target = o_ref.at[c * devices + me]
                if ka or kb:
                    pltpu.make_async_remote_copy(
                        src_ref=source,
                        dst_ref=target,
                        send_sem=out_send,
                        recv_sem=out_recv,
                        device_id=(a, b),
                        device_id_type=MESH,
                    ).start()
                else:
                    pltpu.make_async_copy(source, target, out_local).start()
        return carry

    lax.fori_loop(0, parts, one_part, 0)
    others = arrived.at[:, pl.ds(0, rads - 1)]
    pltpu.make_async_copy(others, others, in_send).wait()
    remote = pl.ds(0, parts * (devices - 1))
    pltpu.make_async_copy(held.at[remote], held.at[remote], out_send).wait()
    pltpu.make_async_copy(o_ref.at[remote], o_ref.at[remote], out_recv).wait()
    own = pl.ds(0, parts)
    pltpu.make_async_copy(held.at[own], o_ref.at[own], out_local).wait()


def on_device(
    rads,
    modes,
    coefficients,
    legendre,
    radial_left_factor,
    radial_right,
    eigen_rates,
    diffusivity,
    slot_order,
    slot_start,
):
    packed, lats = legendre.shape[2:]
    radii = radial_right.shape[1]
    fields, parts_count = coefficients.shape[:2]
    parts = fields * parts_count
    devices = rads * modes
    rows, columns = radii // rads, lats // modes
    smem = pl.BlockSpec(memory_space=pltpu.SMEM)
    vmem = pl.BlockSpec(memory_space=pltpu.VMEM)
    hbm = pl.BlockSpec(memory_space=pltpu.HBM)
    landed = pl.pallas_call(
        functools.partial(whole_kernel, rads, modes, parts_count),
        out_shape=pltpu.VMEM((parts * devices, rows, 2, columns), jnp.bfloat16),
        in_specs=[smem, smem, smem, vmem, hbm, hbm, hbm, hbm],
        out_specs=pl.BlockSpec(memory_space=pl.ANY),
        scratch_shapes=[
            pltpu.VMEM(radial_left_factor.shape, jnp.float32),
            pltpu.VMEM(radial_right.shape, jnp.float32),
            pltpu.VMEM((parts, rows, rads, packed), jnp.bfloat16),
            pltpu.VMEM((parts, rads, rows, packed), jnp.bfloat16),
            pltpu.VMEM((parts, rads, rows, packed), jnp.bfloat16),
            pltpu.VMEM((packed, lats), jnp.bfloat16),
            pltpu.VMEM((2 * radii, packed), jnp.bfloat16),
            pltpu.VMEM((parts * devices, rows, 2, columns), jnp.bfloat16),
            pltpu.SemaphoreType.DMA((parts,)),
            pltpu.SemaphoreType.DMA,
            pltpu.SemaphoreType.DMA((parts,)),
            pltpu.SemaphoreType.DMA((2,)),
            pltpu.SemaphoreType.DMA,
            pltpu.SemaphoreType.DMA,
            pltpu.SemaphoreType.DMA,
            pltpu.SemaphoreType.DMA,
        ],
        compiler_params=pltpu.CompilerParams(
            collective_id=0, has_side_effects=True, vmem_limit_bytes=46 * 2**20
        ),
    )(
        slot_order,
        slot_start,
        diffusivity,
        eigen_rates,
        radial_left_factor,
        radial_right,
        coefficients.reshape(parts, rows, rads, packed),
        legendre.reshape(packed, lats),
    )
    return landed.reshape(fields, parts_count, rads, modes, rows, 2, columns)


def solution(mesh):
    rads, modes = mesh.shape["rad"], mesh.shape["mode"]
    return jax.shard_map(
        functools.partial(on_device, rads, modes),
        mesh=mesh,
        in_specs=(
            P(None, None, "rad", None, "mode", None),
            P("rad", "mode", None, None),
            P(),
            P(),
            P(),
            P(),
            P("rad", "mode", None),
            P("rad", "mode", None),
        ),
        out_specs=P(None, None, None, None, "rad", None, "mode"),
        check_vma=False,
    )
```

```python
import functools
import jax
import jax.numpy as jnp
from jax import lax
from jax.experimental import pallas as pl
from jax.experimental.pallas import tpu as pltpu
from jax.sharding import PartitionSpec as P

DEGREES = 1024
BLOCK = 128
MESH = pl.DeviceIdType.MESH


def peer_rad(my_rad, rads, k):
    half = rads // 2
    near = my_rad // half
    side = near if k < half else 1 - near
    return side * half + lax.rem(my_rad % half + k, half)


def whole_kernel(
    rads,
    modes,
    parts_count,
    order_ref,
    start_ref,
    diffusivity_ref,
    eigen_ref,
    left_hbm,
    right_hbm,
    x_ref,
    legendre_ref,
    o_ref,
    left_ref,
    right_ref,
    entering,
    outgoing,
    arrived,
    polynomial_rows,
    updated,
    held,
    enter_sem,
    in_send,
    in_recv,
    factor_sem,
    legendre_sem,
    out_send,
    out_recv,
    out_local,
):
    my_rad = lax.axis_index("rad")
    my_mode = lax.axis_index("mode")
    devices = rads * modes
    parts = arrived.shape[0]
    packed = arrived.shape[3]
    radii = right_ref.shape[1]
    rows, lats = held.shape[1], held.shape[3]
    me = my_rad * modes + my_mode

    def enter(c):
        return pltpu.make_async_copy(x_ref.at[c], entering.at[c], enter_sem.at[c])

    for c in range(parts):
        enter(c).start()
    fetches = (
        pltpu.make_async_copy(left_hbm, left_ref, factor_sem.at[0]),
        pltpu.make_async_copy(right_hbm, right_ref, factor_sem.at[1]),
        pltpu.make_async_copy(legendre_ref, polynomial_rows, legendre_sem),
    )
    for fetch in fetches:
        fetch.start()
    barrier = pltpu.get_barrier_semaphore()
    for ka in range(rads):
        for kb in range(modes):
            if ka or kb:
                peer = (lax.rem(my_rad + ka, rads), lax.rem(my_mode + kb, modes))
                pl.semaphore_signal(barrier, inc=1, device_id=peer, device_id_type=MESH)

    def turn(c):
        enter(c).wait()
        outgoing[c] = jnp.swapaxes(entering[c], 0, 1)

    turn(0)
    pl.semaphore_wait(barrier, devices - 1)

    def send_part(c, carry):
        @pl.when(c > 0)
        def _():
            turn(c)

        for ka in reversed(range(rads)):
            a = peer_rad(my_rad, rads, ka)
            source = outgoing.at[c, a]
            target = arrived.at[c, my_rad]
            if ka:
                pltpu.make_async_remote_copy(
                    src_ref=source,
                    dst_ref=target,
                    send_sem=in_send,
                    recv_sem=in_recv.at[c],
                    device_id=(a, my_mode),
                    device_id_type=MESH,
                ).start()
            else:
                pltpu.make_async_copy(source, target, in_recv.at[c]).start()
        return carry

    lax.fori_loop(0, parts, send_part, 0)

    position = lax.broadcasted_iota(jnp.int32, (1, packed), 1)
    live = []
    degree = jnp.zeros((1, packed), jnp.int32)
    for s in range(2):
        order = order_ref[0, 0, s]
        start = start_ref[0, 0, s]
        first_degree = BLOCK * (order // BLOCK)
        inside = (position >= start) & (position < start + DEGREES - first_degree)
        row_degree = first_degree + position - start
        degree = degree + jnp.where(inside, row_degree, 0)
        live.append(jnp.where(inside & (row_degree >= order), 1.0, 0.0).astype(jnp.float32))
    degree_level = degree.astype(jnp.float32)
    harmonic = degree_level * (degree_level + 1.0) / (DEGREES * DEGREES)
    covered = jnp.maximum(live[0], live[1])
    row = lax.broadcasted_iota(jnp.int32, (2 * radii, radii), 0)
    column = lax.broadcasted_iota(jnp.int32, (2 * radii, radii), 1)
    doubling = jnp.where(row // 2 == column, 1.0, 0.0).astype(jnp.bfloat16)
    parity = lax.broadcasted_iota(jnp.int32, (2 * radii, packed), 0) % 2
    for fetch in fetches:
        fetch.wait()

    def one_part(c, carry):
        field = c // parts_count
        pltpu.make_async_copy(arrived.at[c], arrived.at[c], in_recv.at[c]).wait()
        rates = eigen_ref[pl.ds(field, 1), :]
        rates = jnp.transpose(jnp.broadcast_to(rates, (128, radii)))[:, 0:1]
        shrink = 1.0 + rates + diffusivity_ref[field] * harmonic
        values = arrived[c].reshape(radii, packed).astype(jnp.float32)
        turned = jnp.dot(
            left_ref[field], values, precision=lax.Precision.HIGHEST, preferred_element_type=jnp.float32
        )
        scaled = turned * (covered / shrink)
        result = jnp.dot(
            right_ref[field], scaled, precision=lax.Precision.HIGHEST, preferred_element_type=jnp.float32
        )
        doubled = jnp.dot(doubling, result.astype(jnp.bfloat16), preferred_element_type=jnp.float32)
        updated[...] = (doubled * jnp.where(parity == 0, live[0], live[1])).astype(jnp.bfloat16)
        for kb in range(modes):
            b = lax.rem(my_mode + kb, modes)
            columns = pl.ds(pl.multiple_of(b * lats, lats), lats)
            summed = jnp.dot(
                updated[...], polynomial_rows[:, columns], preferred_element_type=jnp.float32
            )
            blocks = summed.reshape(rads, rows, 2, lats).astype(jnp.bfloat16)
            for a in range(rads):
                held[(c * modes + kb) * rads + a] = blocks[a]
            for ka in reversed(range(rads)):
                a = peer_rad(my_rad, rads, ka)
                source = held.at[(c * modes + kb) * rads + a]
                target = o_ref.at[c * devices + me]
                if ka or kb:
                    pltpu.make_async_remote_copy(
                        src_ref=source,
                        dst_ref=target,
                        send_sem=out_send,
                        recv_sem=out_recv,
                        device_id=(a, b),
                        device_id_type=MESH,
                    ).start()
                else:
                    pltpu.make_async_copy(source, target, out_local).start()
        return carry

    lax.fori_loop(0, parts, one_part, 0)
    others = arrived.at[:, pl.ds(0, rads - 1)]
    pltpu.make_async_copy(others, others, in_send).wait()
    remote = pl.ds(0, parts * (devices - 1))
    pltpu.make_async_copy(held.at[remote], held.at[remote], out_send).wait()
    pltpu.make_async_copy(o_ref.at[remote], o_ref.at[remote], out_recv).wait()
    own = pl.ds(0, parts)
    pltpu.make_async_copy(held.at[own], o_ref.at[own], out_local).wait()


def on_device(
    rads,
    modes,
    coefficients,
    legendre,
    radial_left_factor,
    radial_right,
    eigen_rates,
    diffusivity,
    slot_order,
    slot_start,
):
    packed, lats = legendre.shape[2:]
    radii = radial_right.shape[1]
    fields, parts_count = coefficients.shape[:2]
    parts = fields * parts_count
    devices = rads * modes
    rows, columns = radii // rads, lats // modes
    smem = pl.BlockSpec(memory_space=pltpu.SMEM)
    vmem = pl.BlockSpec(memory_space=pltpu.VMEM)
    hbm = pl.BlockSpec(memory_space=pltpu.HBM)
    landed = pl.pallas_call(
        functools.partial(whole_kernel, rads, modes, parts_count),
        out_shape=pltpu.VMEM((parts * devices, rows, 2, columns), jnp.bfloat16),
        in_specs=[smem, smem, smem, vmem, hbm, hbm, hbm, hbm],
        out_specs=pl.BlockSpec(memory_space=pl.ANY),
        scratch_shapes=[
            pltpu.VMEM(radial_left_factor.shape, jnp.float32),
            pltpu.VMEM(radial_right.shape, jnp.float32),
            pltpu.VMEM((parts, rows, rads, packed), jnp.bfloat16),
            pltpu.VMEM((parts, rads, rows, packed), jnp.bfloat16),
            pltpu.VMEM((parts, rads, rows, packed), jnp.bfloat16),
            pltpu.VMEM((packed, lats), jnp.bfloat16),
            pltpu.VMEM((2 * radii, packed), jnp.bfloat16),
            pltpu.VMEM((parts * devices, rows, 2, columns), jnp.bfloat16),
            pltpu.SemaphoreType.DMA((parts,)),
            pltpu.SemaphoreType.DMA,
            pltpu.SemaphoreType.DMA((parts,)),
            pltpu.SemaphoreType.DMA((2,)),
            pltpu.SemaphoreType.DMA,
            pltpu.SemaphoreType.DMA,
            pltpu.SemaphoreType.DMA,
            pltpu.SemaphoreType.DMA,
        ],
        compiler_params=pltpu.CompilerParams(
            collective_id=0, has_side_effects=True, vmem_limit_bytes=46 * 2**20
        ),
    )(
        slot_order,
        slot_start,
        diffusivity,
        eigen_rates,
        radial_left_factor,
        radial_right,
        coefficients.reshape(parts, rows, rads, packed),
        legendre.reshape(packed, lats),
    )
    return landed.reshape(fields, parts_count, rads, modes, rows, 2, columns)


def solution(mesh):
    rads, modes = mesh.shape["rad"], mesh.shape["mode"]
    return jax.shard_map(
        functools.partial(on_device, rads, modes),
        mesh=mesh,
        in_specs=(
            P(None, None, "rad", None, "mode", None),
            P("rad", "mode", None, None),
            P(),
            P(),
            P(),
            P(),
            P("rad", "mode", None),
            P("rad", "mode", None),
        ),
        out_specs=P(None, None, None, None, "rad", None, "mode"),
        check_vma=False,
    )
```
